32 devices in a mesh: dp: 8 (over z, y), tensor: 4 (over x, core).
Axes of the slice: x: 2, y: 2, z: 4, core: 2. Of those that a mesh axis runs over, the one named last changes fastest.
Arguments:
- query_act: bfloat16 [8, 1024, 1024], P('dp', None, 'tensor'), may hold values from -6 to 6
- rotated_keys: bfloat16 [8, 1024, 256], P('dp'), may hold values from -6 to 6
- value_input: bfloat16 [8, 1024, 256], P('dp'), may hold values from -6 to 6
- grad_out: bfloat16 [8, 1024, 8192], P('dp', 'tensor'), may hold values from -6 to 6
- out_weight: bfloat16 [1024, 8192], P('tensor', 'dp'), may hold values from -0.1875 to 0.1875
- doc_lengths: int32 [8, 4], P('dp'), may hold values from 1 to 512, 1024 in all within a row
Outputs:
- query_grad: bfloat16 [8, 1024, 1024], P('dp', None, 'tensor')
- key_gradient: bfloat16 [8, 4, 512, 128], P('dp', 'tensor')
- value_gradient: bfloat16 [8, 4, 512, 128], P('dp', 'tensor')
- weight_grad: float32 [1024, 8192], P('tensor', 'dp')
The draws below stay inside these ranges and needn't reach their ends.
All inputs are finite; a program needn't handle non-finite values.
Results may differ from the reference program's by a relative error of at most 0.015.
The reference program's roundings to bfloat16 on the way count: a program that leaves them out, or rounds other values in their place, can miss the bound.
Values may be sent and summed in bfloat16 or wider, within the bound.
A program may use at most 128 MiB of HBM per device.

```python
import math
import jax
import jax.numpy as jnp
import numpy as np
from jax import lax

D = 8192
HEAD_SIZE = 128
SEQUENCE_TOKENS = 1024
NDOCS = 4
SEQUENCE_COUNT = 8
QUERY_HEADS = 8
KEY_VALUE_HEADS = 2


def draw_query_act(key, part):
    array_shape = (SEQUENCE_COUNT, SEQUENCE_TOKENS, QUERY_HEADS * HEAD_SIZE)
    drawn = jnp.clip(jax.random.normal(jax.random.fold_in(key, 1), array_shape, jnp.float32), -6.0, 6.0)
    return drawn.astype(jnp.bfloat16)


def draw_rotated_keys(key, part):
    array_shape = (SEQUENCE_COUNT, SEQUENCE_TOKENS, KEY_VALUE_HEADS * HEAD_SIZE)
    drawn = jnp.clip(jax.random.normal(jax.random.fold_in(key, 3), array_shape, jnp.float32), -6.0, 6.0)
    return drawn.astype(jnp.bfloat16)


def raised(values, key, source, target, parts, factor):
    def block_of(position):
        return (jnp.arange(values.shape[position]) // (values.shape[position] // parts)).reshape((-1,) + (1,) * (values.ndim - 1 - position))

    first = jax.random.permutation(key, parts)[block_of(target)]
    far = (block_of(target) + parts // 2) % parts
    return jnp.where((block_of(source) == first) | (block_of(source) == far), factor * values, values)


def shard_levels(own_key, dims, split, low, high):
    level, own = 1.0, jax.random.fold_in(own_key, 6)
    for dim, parts in split:
        draws = jnp.exp(jax.random.uniform(jax.random.fold_in(own, dim), (parts,), jnp.float32, low / len(split), high / len(split)))
        level = level * jnp.repeat(draws, dims[dim] // parts).reshape([-1 if axis == dim else 1 for axis in range(len(dims))])
    return level


def profile(number_of, total, bound, skew):
    weights = [(1 << 20) // math.isqrt(standing ** skew) + 1 for standing in range(2, number_of + 1)]
    rest, holding = total - bound - (number_of - 1), [1] * (number_of - 1)
    while rest > 0:
        candidates = [i for i in range(number_of - 1) if holding[i] < bound]
        mass, budget = sum([weights[i] for i in candidates]), rest
        for i in candidates:
            extra = min(bound - holding[i], max(1, budget * weights[i] // mass), rest)
            holding[i] = holding[i] + extra
            rest = rest - extra
    return np.array([bound] + holding)


def uneven(key, number_of, total, reach, slope):
    if number_of == 2:
        one = jax.random.randint(key, (), max(1, total - reach), min(reach, total - 1) + 1)
        return jnp.stack([one, total - one])
    tallies = jnp.asarray(profile(number_of, total, reach, slope), jnp.int32)
    pairs = (number_of - 1) // 2
    giver, taker = tallies[1:1 + 2 * pairs:2], tallies[2:2 + 2 * pairs:2]
    margin = jnp.minimum(giver - 1, reach - taker)
    shifted = jax.random.randint(jax.random.fold_in(key, 1), (pairs,), 0, 1 << 20) % (margin + 1)
    tallies = tallies.at[1:1 + 2 * pairs:2].set(giver - shifted).at[2:2 + 2 * pairs:2].set(taker + shifted)
    return tallies[jax.random.permutation(jax.random.fold_in(key, 2), number_of)]


def bell_draw(own_key, shape, deviation, limit, pieces=(), held_as=jnp.bfloat16):
    loudness = shard_levels(own_key, shape, pieces, -0.22, 0.18) if pieces else 1.0
    array = jax.random.normal(own_key, shape, jnp.float32) * deviation * loudness
    return jnp.minimum(jnp.maximum(array, -limit), limit).astype(held_as)


def gaussian_with(stream_key, dims, scale, bound, shards, heavy, kind=jnp.bfloat16):
    array = scale * jax.random.normal(stream_key, dims, jnp.float32)
    if shards:
        array = array * shard_levels(stream_key, dims, shards, -0.22, 0.18)
    return jnp.clip(raised(array, jax.random.fold_in(stream_key, 3), *heavy), -bound, bound).astype(kind)


def setup_inputs(seed: int = 0) -> dict:
    keys = jax.random.split(jax.random.key(seed), 7)
    query_act = draw_query_act(jax.random.fold_in(keys[6], 71), 0)
    rotated_keys = draw_rotated_keys(jax.random.fold_in(keys[6], 71), 0)
    value_input = bell_draw(keys[2], (SEQUENCE_COUNT, SEQUENCE_TOKENS, KEY_VALUE_HEADS * HEAD_SIZE), 1.0, 6.0, ((0, 8),))
    grad_out = gaussian_with(keys[3], (SEQUENCE_COUNT, SEQUENCE_TOKENS, D), 1.0, 6.0, ((0, 8), (1, 4)), (0, 2, 8, 2.0))
    out_weight = bell_draw(keys[4], (QUERY_HEADS * HEAD_SIZE, D), (QUERY_HEADS * HEAD_SIZE) ** -0.5, 0.1875, ((0, 4), (1, 8)))
    doc_lengths = jax.vmap(lambda own: uneven(own, NDOCS, SEQUENCE_TOKENS, SEQUENCE_TOKENS // 2, 2))(jax.random.split(keys[5], SEQUENCE_COUNT)).reshape((SEQUENCE_COUNT, NDOCS)).astype(jnp.int32)
    return dict(query_act=query_act, rotated_keys=rotated_keys, value_input=value_input, grad_out=grad_out, out_weight=out_weight, doc_lengths=doc_lengths)


def doc_mask(lengths):
    doc_ends = jnp.cumsum(lengths).astype(jnp.int32)
    positions = jnp.arange(SEQUENCE_TOKENS, dtype=jnp.int32)
    doc_ids = jnp.sum((positions[:, None] >= doc_ends[None, :]).astype(jnp.int32), axis=1)
    return (positions[None, :] <= positions[:, None]) & (doc_ids[:, None] == doc_ids[None, :])


def one_sequence(out_weight, sequence):
    query_act, rotated_keys, value_input, grad_out, lengths = sequence
    score_scale = HEAD_SIZE ** -0.5
    query_group_width = QUERY_HEADS // KEY_VALUE_HEADS
    allowed = doc_mask(lengths)
    query_float32 = query_act.astype(jnp.float32).reshape(SEQUENCE_TOKENS, QUERY_HEADS, HEAD_SIZE).transpose(1, 0, 2)
    key_float32 = jnp.repeat(rotated_keys.astype(jnp.float32).reshape(SEQUENCE_TOKENS, KEY_VALUE_HEADS, HEAD_SIZE).transpose(1, 0, 2), query_group_width, axis=0)
    value_float32 = jnp.repeat(value_input.astype(jnp.float32).reshape(SEQUENCE_TOKENS, KEY_VALUE_HEADS, HEAD_SIZE).transpose(1, 0, 2), query_group_width, axis=0)
    scores = jnp.einsum('hqd,hkd->hqk', query_float32, key_float32) * score_scale
    scores = jnp.where(allowed[None], scores, -jnp.inf)
    row_max = jnp.max(scores, axis=-1, keepdims=True)
    log_total = row_max + jnp.log(jnp.sum(jnp.exp(scores - row_max), axis=-1, keepdims=True))
    probs = jnp.exp(scores - log_total)
    probability_narrow = lax.optimization_barrier(probs.astype(jnp.bfloat16)).astype(jnp.float32)
    attn_out = jnp.einsum('hqk,hkd->hqd', probability_narrow, value_float32).astype(jnp.bfloat16)
    out_flat = attn_out.transpose(1, 0, 2).reshape(SEQUENCE_TOKENS, QUERY_HEADS * HEAD_SIZE)
    out_grad = jnp.dot(grad_out, out_weight.T, preferred_element_type=jnp.float32).astype(jnp.bfloat16)
    weight_part = jnp.dot(out_flat.T, grad_out, preferred_element_type=jnp.float32)
    gradient_float32 = lax.optimization_barrier(out_grad).astype(jnp.float32).reshape(SEQUENCE_TOKENS, QUERY_HEADS, HEAD_SIZE).transpose(1, 0, 2)
    out_f32 = lax.optimization_barrier(attn_out).astype(jnp.float32)
    dprobs = jnp.einsum('hqd,hkd->hqk', gradient_float32, value_float32)
    row_delta = jnp.sum(gradient_float32 * out_f32, axis=-1, keepdims=True)
    score_gradient = lax.optimization_barrier((probs * (dprobs - row_delta) * score_scale).astype(jnp.bfloat16)).astype(jnp.float32)
    query_grad = jnp.einsum('hqk,hkd->hqd', score_gradient, key_float32).astype(jnp.bfloat16)
    query_grad = query_grad.transpose(1, 0, 2).reshape(SEQUENCE_TOKENS, QUERY_HEADS * HEAD_SIZE)
    key_head_rows = jnp.einsum('auf,aur->afr', score_gradient, query_float32).reshape(KEY_VALUE_HEADS, query_group_width, SEQUENCE_TOKENS, HEAD_SIZE)
    value_head_rows = jnp.einsum('auf,aur->afr', probability_narrow, gradient_float32).reshape(KEY_VALUE_HEADS, query_group_width, SEQUENCE_TOKENS, HEAD_SIZE)
    key_gradient = jnp.sum(key_head_rows, axis=1).astype(jnp.bfloat16).reshape(2 * KEY_VALUE_HEADS, SEQUENCE_TOKENS // 2, HEAD_SIZE)
    value_gradient = jnp.sum(value_head_rows, axis=1).astype(jnp.bfloat16).reshape(2 * KEY_VALUE_HEADS, SEQUENCE_TOKENS // 2, HEAD_SIZE)
    return weight_part, (query_grad, key_gradient, value_gradient)


def reference(query_act, rotated_keys, value_input, grad_out, out_weight, doc_lengths):
    def scan_step(grad_sum, sequence):
        weight_part, others = one_sequence(out_weight, sequence)
        return grad_sum + weight_part, others

    initial = jnp.zeros((QUERY_HEADS * HEAD_SIZE, D), jnp.float32)
    weight_grad, stacked = lax.scan(scan_step, initial, (query_act, rotated_keys, value_input, grad_out, doc_lengths))
    query_grad, key_gradient, value_gradient = stacked
    return query_grad, key_gradient, value_gradient, weight_grad
```

```python
import functools

import jax
import jax.numpy as jnp
from jax import lax
from jax.experimental import pallas as pl
from jax.experimental.pallas import tpu as pltpu
from jax.sharding import PartitionSpec as P

HEAD_SIZE = 128


MESH = pl.DeviceIdType.MESH


def ring_place(index, count):
    odd = index % 2
    return (1 - odd) * (index // 2) + odd * (count - 1 - index // 2)


def ring_index(place, count):
    back = place // (count // 2)
    return (1 - back) * (2 * place) + back * (2 * (count - 1 - place) + 1)


def exchange_kernel(
    dp_count,
    tensor_count,
    grad_ref,
    weight_ref,
    out_t_ref,
    out_grad_ref,
    weight_grad_ref,
    grads,
    weights,
    sums_out,
    sums_in,
    accum,
    own_sem,
    own_weight_sem,
    near_send,
    near_recv,
    far_send,
    far_recv,
    pass_send,
    pass_recv,
    weight_send,
    weight_recv,
    sum_send,
    sum_recv,
):
    dp_index = lax.axis_index("dp")
    tensor_index = lax.axis_index("tensor")
    chip_count = tensor_count // 2
    chip, core = tensor_index // 2, tensor_index % 2
    partner = chip * 2 + 1 - core
    place = ring_place(dp_index, dp_count)
    ring = (
        ring_index((place + 1) % dp_count, dp_count),
        ring_index((place + dp_count - 1) % dp_count, dp_count),
    )
    rows = grad_ref.shape[0]
    half = weight_ref.shape[1] // 2
    last = dp_count - 1
    far_chips = [(chip + away) % chip_count for away in range(1, chip_count)]

    def place_rows(index):
        return pl.ds(pl.multiple_of(index * rows, rows), rows)

    def columns(side, step):
        if side == 0:
            owner = ring_index((place + 2 * dp_count - 1 - step) % dp_count, dp_count)
        else:
            owner = ring_index((place + 1 + step) % dp_count, dp_count)
        return pl.ds(pl.multiple_of(owner * (2 * half) + side * half, half), half)

    def own_copy(side, step):
        return pltpu.make_async_copy(
            grad_ref.at[:, columns(side, step)],
            grads.at[side, step, place_rows(tensor_index)],
            own_sem.at[side, step],
        )

    def own_weight(side):
        return pltpu.make_async_copy(
            weight_ref.at[:, pl.ds(side * half, half)],
            weights.at[side, last],
            own_weight_sem.at[side],
        )

    def near_copy(side, step):
        return pltpu.make_async_remote_copy(
            grad_ref.at[:, columns(side, step)],
            grads.at[side, step, place_rows(tensor_index)],
            near_send.at[side, step],
            near_recv.at[side, step],
            device_id=(dp_index, partner),
            device_id_type=MESH,
        )

    def far_copy(away, side, step):
        return pltpu.make_async_remote_copy(
            grad_ref.at[:, columns(side, step)],
            grads.at[side, step, place_rows(tensor_index)],
            far_send.at[away, side, step],
            far_recv.at[away, side, step],
            device_id=(dp_index, far_chips[away] * 2 + core),
            device_id_type=MESH,
        )

    def pass_copy(away, side, step):
        source = (chip + chip_count - 1 - away) % chip_count * 2 + core
        block = grads.at[side, step, place_rows(source)]
        return pltpu.make_async_remote_copy(
            block,
            block,
            pass_send.at[away, side, step],
            pass_recv.at[away, side, step],
            device_id=(dp_index, partner),
            device_id_type=MESH,
        )

    def weight_copy(side, hop):
        if isinstance(hop, int) and hop == 0:
            source = weight_ref.at[:, pl.ds(side * half, half)]
        else:
            source = weights.at[side, hop - 1]
        return pltpu.make_async_remote_copy(
            source,
            weights.at[side, hop],
            weight_send.at[side, hop],
            weight_recv.at[side, hop],
            device_id=(ring[side], tensor_index),
            device_id_type=MESH,
        )

    def sum_copy(side, step):
        return pltpu.make_async_remote_copy(
            sums_out.at[side, step],
            sums_in.at[side, step],
            sum_send.at[side, step],
            sum_recv.at[side, step],
            device_id=(ring[side], tensor_index),
            device_id_type=MESH,
        )

    targets = [(dp_index, partner), (ring[0], tensor_index), (ring[1], tensor_index)]
    targets += [(dp_index, other * 2 + core) for other in far_chips]
    barrier = pltpu.get_barrier_semaphore()
    for target in targets:
        pl.semaphore_signal(barrier, inc=1, device_id=target, device_id_type=MESH)
    pl.semaphore_wait(barrier, len(targets))

    for side in (0, 1):
        weight_copy(side, 0).start()
        own_weight(side).start()

    @pl.loop(0, dp_count)
    def _(step):
        for side in (0, 1):
            for away in range(chip_count - 1):
                far_copy(away, side, step).start()

    @pl.loop(0, dp_count)
    def _(step):
        for side in (0, 1):
            near_copy(side, step).start()
            own_copy(side, step).start()

    accum[...] = jnp.zeros_like(accum)
    for side in (0, 1):
        weight_copy(side, 0).wait_recv()
        weight_copy(side, 1).start()

    def run(step, first, final, forward):
        for side in (0, 1):
            if forward is None:
                pass
            elif forward:
                weight_copy(side, step + 1).wait_recv()
                weight_copy(side, step + 2).start()
            else:
                weight_copy(side, step + 1).wait_recv()
        for side in (0, 1):
            for away in range(chip_count - 1):
                far_copy(away, side, step).wait_recv()
                pass_copy(away, side, step).start()
        for side in (0, 1):
            own_copy(side, step).wait()
            near_copy(side, step).wait_recv()
            if final:
                own_weight(side).wait()
        for side in (0, 1):
            for away in range(chip_count - 1):
                pass_copy(away, side, step).wait_recv()
            part = jnp.dot(
                out_t_ref[...], grads[side, step], preferred_element_type=jnp.float32
            )
            if not first:
                sum_copy(side, step - 1).wait_recv()
                part = part + sums_in[side, step - 1].astype(jnp.float32)
            if final:
                weight_grad_ref[:, side * half : (side + 1) * half] = part
            else:
                sums_out[side, step] = part.astype(jnp.bfloat16)
                sum_copy(side, step).start()
        both = (((1,), (1,)), ((), ()))
        total = accum[...]
        for side in (0, 1):
            total += lax.dot_general(
                grads[side, step], weights[side, step], both, preferred_element_type=jnp.float32
            )
        if final:
            out_grad_ref[...] = total.astype(jnp.bfloat16)
        else:
            accum[...] = total

    run(0, True, False, True)

    @pl.loop(1, dp_count - 3)
    def _(step):
        run(step, False, False, True)

    run(dp_count - 3, False, False, False)
    run(dp_count - 2, False, False, None)
    run(dp_count - 1, False, True, None)

    @pl.loop(0, dp_count)
    def _(step):
        for side in (0, 1):
            near_copy(side, step).wait_send()
            for away in range(chip_count - 1):
                far_copy(away, side, step).wait_send()
                pass_copy(away, side, step).wait_send()

    @pl.loop(1, dp_count - 1)
    def _(step):
        for side in (0, 1):
            weight_copy(side, step).wait_send()
            sum_copy(side, step).wait_send()

    for side in (0, 1):
        weight_copy(side, 0).wait_send()
        sum_copy(side, 0).wait_send()


def exchange(grad_rows, out_weight, out_t):
    dp_count, tensor_count = lax.axis_size("dp"), lax.axis_size("tensor")
    far = tensor_count // 2 - 1
    rows = grad_rows.shape[0]
    seq_len = rows * tensor_count
    depth, width = out_weight.shape
    half = width // 2
    dma = pltpu.SemaphoreType.DMA
    vmem = pl.BlockSpec(memory_space=pltpu.VMEM)
    return pl.pallas_call(
        functools.partial(exchange_kernel, dp_count, tensor_count),
        out_shape=(
            jax.ShapeDtypeStruct((seq_len, depth), jnp.bfloat16),
            jax.ShapeDtypeStruct((depth, width), jnp.float32),
        ),
        in_specs=[pl.BlockSpec(memory_space=pl.ANY), pl.BlockSpec(memory_space=pl.ANY), vmem],
        out_specs=(vmem, vmem),
        scratch_shapes=[
            pltpu.VMEM((2, dp_count, seq_len, half), jnp.bfloat16),
            pltpu.VMEM((2, dp_count, depth, half), jnp.bfloat16),
            pltpu.VMEM((2, dp_count - 1, depth, half), jnp.bfloat16),
            pltpu.VMEM((2, dp_count - 1, depth, half), jnp.bfloat16),
            pltpu.VMEM((seq_len, depth), jnp.float32),
            dma((2, dp_count)),
            dma((2,)),
            dma((2, dp_count)),
            dma((2, dp_count)),
            dma((far, 2, dp_count)),
            dma((far, 2, dp_count)),
            dma((far, 2, dp_count)),
            dma((far, 2, dp_count)),
            dma((2, dp_count - 1)),
            dma((2, dp_count - 1)),
            dma((2, dp_count - 1)),
            dma((2, dp_count - 1)),
        ],
        compiler_params=pltpu.CompilerParams(
            collective_id=0, has_side_effects=True, vmem_limit_bytes=60 * 1024 * 1024
        ),
        name="exchange",
    )(grad_rows, out_weight, out_t)


def swapped(value, axis, apart):
    mask = 2**apart
    pairs = [(source, source ^ mask) for source in range(lax.axis_size(axis))]
    return lax.ppermute(value, axis, pairs)


def shards(query_act, rotated_keys, value_input, grad_out, out_weight, doc_lengths):
    score_scale = HEAD_SIZE ** (-0.5)
    tensor_index = lax.axis_index("tensor")
    kv_group = tensor_index // 2
    own_half = tensor_index % 2
    seq_len = query_act.shape[1]
    head_count = query_act.shape[2] // HEAD_SIZE
    query_heads = query_act[0].reshape(seq_len, head_count, HEAD_SIZE).transpose(1, 0, 2)
    key_rows = lax.dynamic_slice_in_dim(rotated_keys[0], kv_group * HEAD_SIZE, HEAD_SIZE, 1)
    value_rows = lax.dynamic_slice_in_dim(value_input[0], kv_group * HEAD_SIZE, HEAD_SIZE, 1)
    doc_ends = jnp.cumsum(doc_lengths[0])
    positions = jnp.arange(seq_len, dtype=jnp.int32)
    doc_ids = jnp.sum((positions[:, None] >= doc_ends[None, :]).astype(jnp.int32), axis=1)
    block_rows = min(512, seq_len)
    block_count = seq_len // block_rows

    def key_reach():
        return seq_len

    def masked_scores(block_idx, key_span):
        first = block_idx * block_rows
        query_block = query_heads[:, first : first + block_rows]
        scores = (
            jnp.einsum("hqd,kd->hqk", query_block, key_rows, preferred_element_type=jnp.float32)
            * score_scale
        )
        allowed = (positions[None, :key_span] <= positions[first : first + block_rows, None]) & (
            doc_ids[None, :key_span] == doc_ids[first : first + block_rows, None]
        )
        return jnp.where(allowed[None], scores, -jnp.inf)

    totals_list = []
    outputs_list = []
    for block_idx in range(block_count):
        key_span = key_reach()
        scores = masked_scores(block_idx, key_span)
        row_max = jnp.max(scores, axis=-1, keepdims=True)
        log_total = row_max + jnp.log(jnp.sum(jnp.exp(scores - row_max), axis=-1, keepdims=True))
        prob_bf16 = jnp.exp(scores - log_total).astype(jnp.bfloat16)
        outputs_list.append(
            jnp.einsum(
                "hqk,kd->hqd", prob_bf16, value_rows, preferred_element_type=jnp.float32
            ).astype(jnp.bfloat16)
        )
        totals_list.append(log_total)
    attn_out = jnp.concatenate(outputs_list, axis=1)
    out_flat = attn_out.transpose(1, 0, 2).reshape(seq_len, head_count * HEAD_SIZE)
    out_grad, weight_grad = exchange(grad_out[0], out_weight, out_flat.T)
    grad_heads = out_grad.reshape(seq_len, head_count, HEAD_SIZE).transpose(1, 0, 2)
    key_accum = jnp.zeros((seq_len, HEAD_SIZE), jnp.float32)
    value_accum = jnp.zeros((seq_len, HEAD_SIZE), jnp.float32)
    query_list = []
    for block_idx in range(block_count):
        key_span = key_reach()
        first = block_idx * block_rows
        scores = masked_scores(block_idx, key_span)
        prob_block = jnp.exp(scores - totals_list[block_idx])
        prob_bf16 = prob_block.astype(jnp.bfloat16)
        grad_block = grad_heads[:, first : first + block_rows]
        out_block = attn_out[:, first : first + block_rows]
        query_block = query_heads[:, first : first + block_rows]
        dprobs = jnp.einsum(
            "hqd,kd->hqk", grad_block, value_rows, preferred_element_type=jnp.float32
        )
        row_delta = jnp.sum(
            grad_block.astype(jnp.float32) * out_block.astype(jnp.float32), axis=-1, keepdims=True
        )
        score_gradient = (prob_block * (dprobs - row_delta) * score_scale).astype(jnp.bfloat16)
        query_list.append(
            jnp.einsum(
                "hqk,kd->hqd", score_gradient, key_rows, preferred_element_type=jnp.float32
            ).astype(jnp.bfloat16)
        )
        key_accum = key_accum.at[:key_span].add(
            jnp.einsum(
                "hqk,hqd->kd", score_gradient, query_block, preferred_element_type=jnp.float32
            )
        )
        value_accum = value_accum.at[:key_span].add(
            jnp.einsum("hqk,hqd->kd", prob_bf16, grad_block, preferred_element_type=jnp.float32)
        )
    query_grad = (
        jnp.concatenate(query_list, axis=1)
        .transpose(1, 0, 2)
        .reshape(1, seq_len, head_count * HEAD_SIZE)
    )
    half_rows = seq_len // 2
    other_start = (1 - own_half) * half_rows
    outgoing = (
        lax.dynamic_slice_in_dim(key_accum, other_start, half_rows, 0),
        lax.dynamic_slice_in_dim(value_accum, other_start, half_rows, 0),
    )
    partner = swapped((outgoing[0], outgoing[1]), "tensor", 0)
    key_mine = lax.dynamic_slice_in_dim(key_accum, own_half * half_rows, half_rows, 0) + partner[0]
    value_mine = (
        lax.dynamic_slice_in_dim(value_accum, own_half * half_rows, half_rows, 0) + partner[1]
    )
    key_gradient = key_mine.astype(jnp.bfloat16).reshape(1, 1, half_rows, HEAD_SIZE)
    value_gradient = value_mine.astype(jnp.bfloat16).reshape(1, 1, half_rows, HEAD_SIZE)
    return (query_grad, key_gradient, value_gradient, weight_grad)


def solution(mesh):
    placed = (
        P("dp", None, "tensor"),
        P("dp", None, None),
        P("dp", None, None),
        P("dp", "tensor", None),
        P("tensor", "dp"),
        P("dp", None),
    )
    return jax.shard_map(
        shards,
        mesh=mesh,
        in_specs=placed,
        out_specs=(
            P("dp", None, "tensor"),
            P("dp", "tensor", None, None),
            P("dp", "tensor", None, None),
            P("tensor", "dp"),
        ),
        check_vma=False,
    )
```

```python
import functools

import jax
import jax.numpy as jnp
from jax import lax
from jax.experimental import pallas as pl
from jax.experimental.pallas import tpu as pltpu
from jax.sharding import PartitionSpec as P

HEAD_SIZE = 128


MESH = pl.DeviceIdType.MESH


def ring_place(index, count):
    odd = index % 2
    return (1 - odd) * (index // 2) + odd * (count - 1 - index // 2)


def ring_index(place, count):
    back = place // (count // 2)
    return (1 - back) * (2 * place) + back * (2 * (count - 1 - place) + 1)


def exchange_kernel(
    dp_count,
    tensor_count,
    grad_ref,
    weight_ref,
    query_ref,
    key_ref,
    value_ref,
    lengths_ref,
    query_grad_ref,
    key_grad_ref,
    value_grad_ref,
    weight_grad_ref,
    grads,
    weights,
    sums_out,
    sums_in,
    accum,
    probs,
    outs,
    outs_t,
    kv_grads,
    kv_in,
    own_sem,
    own_weight_sem,
    near_send,
    near_recv,
    far_send,
    far_recv,
    pass_send,
    pass_recv,
    weight_send,
    weight_recv,
    sum_send,
    sum_recv,
    kv_send,
    kv_recv,
):
    dp_index = lax.axis_index("dp")
    tensor_index = lax.axis_index("tensor")
    chip_count = tensor_count // 2
    chip, core = tensor_index // 2, tensor_index % 2
    partner = chip * 2 + 1 - core
    place = ring_place(dp_index, dp_count)
    ring = (
        ring_index((place + 1) % dp_count, dp_count),
        ring_index((place + dp_count - 1) % dp_count, dp_count),
    )
    rows = grad_ref.shape[0]
    half = weight_ref.shape[1] // 2
    last = dp_count - 1
    seq_len, depth = query_ref.shape
    heads = depth // HEAD_SIZE
    half_rows = seq_len // 2
    score_scale = HEAD_SIZE ** (-0.5)
    lead = min(2, dp_count - 2)
    kv_columns = pl.ds(pl.multiple_of(tensor_index // 2 * HEAD_SIZE, HEAD_SIZE), HEAD_SIZE)
    far_chips = [(chip + away) % chip_count for away in range(1, chip_count)]

    def place_rows(index):
        return pl.ds(pl.multiple_of(index * rows, rows), rows)

    def columns(side, step):
        if side == 0:
            owner = ring_index((place + 2 * dp_count - 1 - step) % dp_count, dp_count)
        else:
            owner = ring_index((place + 1 + step) % dp_count, dp_count)
        return pl.ds(pl.multiple_of(owner * (2 * half) + side * half, half), half)

    def own_copy(side, step):
        return pltpu.make_async_copy(
            grad_ref.at[:, columns(side, step)],
            grads.at[side, step, place_rows(tensor_index)],
            own_sem.at[side, step],
        )

    def own_weight(side):
        return pltpu.make_async_copy(
            weight_ref.at[:, pl.ds(side * half, half)],
            weights.at[side, last],
            own_weight_sem.at[side],
        )

    def near_copy(side, step):
        return pltpu.make_async_remote_copy(
            grad_ref.at[:, columns(side, step)],
            grads.at[side, step, place_rows(tensor_index)],
            near_send.at[side, step],
            near_recv.at[side, step],
            device_id=(dp_index, partner),
            device_id_type=MESH,
        )

    def far_copy(away, side, step):
        return pltpu.make_async_remote_copy(
            grad_ref.at[:, columns(side, step)],
            grads.at[side, step, place_rows(tensor_index)],
            far_send.at[away, side, step],
            far_recv.at[away, side, step],
            device_id=(dp_index, far_chips[away] * 2 + core),
            device_id_type=MESH,
        )

    def pass_copy(away, side, step):
        source = (chip + chip_count - 1 - away) % chip_count * 2 + core
        block = grads.at[side, step, place_rows(source)]
        return pltpu.make_async_remote_copy(
            block,
            block,
            pass_send.at[away, side, step],
            pass_recv.at[away, side, step],
            device_id=(dp_index, partner),
            device_id_type=MESH,
        )

    def weight_copy(side, hop):
        if isinstance(hop, int) and hop == 0:
            source = weight_ref.at[:, pl.ds(side * half, half)]
        else:
            source = weights.at[side, hop - 1]
        return pltpu.make_async_remote_copy(
            source,
            weights.at[side, hop],
            weight_send.at[side, hop],
            weight_recv.at[side, hop],
            device_id=(ring[side], tensor_index),
            device_id_type=MESH,
        )

    def sum_copy(side, step):
        return pltpu.make_async_remote_copy(
            sums_out.at[side, step],
            sums_in.at[side, step],
            sum_send.at[side, step],
            sum_recv.at[side, step],
            device_id=(ring[side], tensor_index),
            device_id_type=MESH,
        )

    targets = [(dp_index, partner), (ring[0], tensor_index), (ring[1], tensor_index)]
    targets += [(dp_index, other * 2 + core) for other in far_chips]
    barrier = pltpu.get_barrier_semaphore()
    for target in targets:
        pl.semaphore_signal(barrier, inc=1, device_id=target, device_id_type=MESH)
    pl.semaphore_wait(barrier, len(targets))

    for side in (0, 1):
        weight_copy(side, 0).start()
        own_weight(side).start()

    @pl.loop(0, dp_count)
    def _(step):
        for side in (0, 1):
            for away in range(chip_count - 1):
                far_copy(away, side, step).start()

    @pl.loop(0, dp_count)
    def _(step):
        for side in (0, 1):
            near_copy(side, step).start()
            own_copy(side, step).start()

    kv_copy = pltpu.make_async_remote_copy(
        kv_grads.at[:, pl.ds(pl.multiple_of((1 - core) * half_rows, half_rows), half_rows)],
        kv_in,
        kv_send,
        kv_recv,
        device_id=(dp_index, partner),
        device_id_type=MESH,
    )
    accum[...] = jnp.zeros_like(accum)
    kv_grads[...] = jnp.zeros_like(kv_grads)
    nt = (((1,), (1,)), ((), ()))
    tn = (((0,), (0,)), ((), ()))

    def dot(left, right, dims):
        return lax.dot_general(left, right, dims, preferred_element_type=jnp.float32)

    def forward(block, size):
        here = pl.ds(pl.multiple_of(block * size, size), size)
        query_places = block * size + lax.broadcasted_iota(jnp.int32, (size, 1), 0)
        key_places = lax.broadcasted_iota(jnp.int32, (size, seq_len), 1)
        doc_start = jnp.zeros((size, 1), jnp.int32)
        doc_end = jnp.int32(0)
        for doc in range(lengths_ref.shape[1]):
            doc_end = doc_end + lengths_ref[0, doc]
            doc_start = jnp.where(query_places >= doc_end, doc_end, doc_start)
        allowed = (key_places >= doc_start) & (key_places <= query_places)
        keys, values = key_ref[:, kv_columns], value_ref[:, kv_columns]
        for head in range(heads):
            lanes = slice(head * HEAD_SIZE, (head + 1) * HEAD_SIZE)
            scores = dot(query_ref[here, lanes], keys, nt) * score_scale
            scores = jnp.where(allowed, scores, -jnp.inf)
            row_max = jnp.max(scores, axis=1, keepdims=True)
            total = jnp.sum(jnp.exp(scores - row_max), axis=1, keepdims=True)
            prob = jnp.exp(scores - (row_max + jnp.log(total)))
            probs[head, here] = prob
            out = jnp.dot(prob.astype(jnp.bfloat16), values, preferred_element_type=jnp.float32)
            outs[here, lanes] = out.astype(jnp.bfloat16)
            outs_t[lanes, here] = out.T.astype(jnp.bfloat16)

    def backward(block):
        here = place_rows(block)
        keys, values = key_ref[:, kv_columns], value_ref[:, kv_columns]
        for head in range(heads):
            lanes = slice(head * HEAD_SIZE, (head + 1) * HEAD_SIZE)
            grad = accum[here, lanes].astype(jnp.bfloat16)
            delta = jnp.sum(
                grad.astype(jnp.float32) * outs[here, lanes].astype(jnp.float32), axis=1, keepdims=True
            )
            prob = probs[head, here]
            dscore = (prob * (dot(grad, values, nt) - delta) * score_scale).astype(jnp.bfloat16)
            query_grad_ref[here, lanes] = jnp.dot(
                dscore, keys, preferred_element_type=jnp.float32
            ).astype(jnp.bfloat16)
            kv_grads[0] += dot(dscore, query_ref[here, lanes], tn)
            kv_grads[1] += dot(prob.astype(jnp.bfloat16), grad, tn)

    def project(owner_chip, step):
        here = pl.ds(pl.multiple_of(owner_chip * (2 * rows), 2 * rows), 2 * rows)
        total = accum[here]
        for side in (0, 1):
            total += dot(grads[side, step, here], weights[side, step], nt)
        accum[here] = total

    def local_step(step):
        for side in (0, 1):
            own_copy(side, step).wait()
            near_copy(side, step).wait_recv()
        project(chip, step)

    def weight_step(hop, send):
        for side in (0, 1):
            weight_copy(side, hop).wait_recv()
            if send:
                weight_copy(side, hop + 1).start()

    def far_step(step):
        for side in (0, 1):
            for away in range(chip_count - 1):
                far_copy(away, side, step).wait_recv()
                pass_copy(away, side, step).start()
        for side in (0, 1):
            for away in range(chip_count - 1):
                pass_copy(away, side, step).wait_recv()

    def sum_step(step, first, final):
        for side in (0, 1):
            part = jnp.dot(
                outs_t[...], grads[side, step], preferred_element_type=jnp.float32
            )
            if not first:
                sum_copy(side, step - 1).wait_recv()
                part = part + sums_in[side, step - 1].astype(jnp.float32)
            if final:
                weight_grad_ref[:, side * half : (side + 1) * half] = part
            else:
                sums_out[side, step] = part.astype(jnp.bfloat16)
                sum_copy(side, step).start()

    def far_project(step):
        for other in far_chips:
            project(other, step)

    block_rows = min(256, seq_len)
    blocks = seq_len // block_rows

    @pl.loop(0, blocks // 2)
    def _(block):
        forward(block, block_rows)

    weight_step(0, dp_count > 2)

    @pl.loop(blocks // 2, blocks)
    def _(block):
        forward(block, block_rows)

    for hop in range(1, lead):
        weight_step(hop, hop < last - 1)
    for side in (0, 1):
        own_weight(side).wait()
    local_step(last)
    for step in range(lead):
        local_step(step)

    def step_with_weights(step, first, send):
        weight_step(step + lead, send)
        local_step(step + lead)
        far_step(step)
        sum_step(step, first, False)
        far_project(step)

    step_with_weights(0, True, lead < last - 1)

    @pl.loop(1, last - 1 - lead)
    def _(step):
        step_with_weights(step, False, True)

    if last - 1 - lead > 0:
        step_with_weights(last - 1 - lead, False, False)

    for step in range(last - lead, last):
        far_step(step)
        sum_step(step, False, False)
        far_project(step)
        if step == last - lead:

            @pl.loop(0, 2)
            def _(block):
                backward(chip * 2 + block)

    far_step(last)
    far_project(last)

    @pl.loop(0, tensor_count - 2)
    def _(block):
        backward((chip * 2 + 2 + block) % tensor_count)

    kv_copy.start()
    sum_step(last, False, True)
    kv_copy.wait()
    mine = pl.ds(pl.multiple_of(core * half_rows, half_rows), half_rows)
    key_grad_ref[...] = (kv_grads[0, mine] + kv_in[0]).astype(jnp.bfloat16)
    value_grad_ref[...] = (kv_grads[1, mine] + kv_in[1]).astype(jnp.bfloat16)

    @pl.loop(0, dp_count)
    def _(step):
        for side in (0, 1):
            near_copy(side, step).wait_send()
            for away in range(chip_count - 1):
                far_copy(away, side, step).wait_send()
                pass_copy(away, side, step).wait_send()

    @pl.loop(1, dp_count - 1)
    def _(step):
        for side in (0, 1):
            weight_copy(side, step).wait_send()
            sum_copy(side, step).wait_send()

    for side in (0, 1):
        weight_copy(side, 0).wait_send()
        sum_copy(side, 0).wait_send()


def shards(query_act, rotated_keys, value_input, grad_out, out_weight, doc_lengths):
    dp_count, tensor_count = lax.axis_size("dp"), lax.axis_size("tensor")
    far = tensor_count // 2 - 1
    seq_len = query_act.shape[1]
    depth, width = out_weight.shape
    half = width // 2
    dma = pltpu.SemaphoreType.DMA
    vmem = pl.BlockSpec(memory_space=pltpu.VMEM)
    anywhere = pl.BlockSpec(memory_space=pl.ANY)
    kv_shape = jax.ShapeDtypeStruct((seq_len // 2, HEAD_SIZE), jnp.bfloat16)
    query_grad, key_grad, value_grad, weight_grad = pl.pallas_call(
        functools.partial(exchange_kernel, dp_count, tensor_count),
        out_shape=(
            jax.ShapeDtypeStruct((seq_len, depth), jnp.bfloat16),
            kv_shape,
            kv_shape,
            jax.ShapeDtypeStruct((depth, width), jnp.float32),
        ),
        in_specs=[
            anywhere,
            anywhere,
            vmem,
            vmem,
            vmem,
            pl.BlockSpec(memory_space=pltpu.SMEM),
        ],
        out_specs=(vmem, vmem, vmem, vmem),
        scratch_shapes=[
            pltpu.VMEM((2, dp_count, seq_len, half), jnp.bfloat16),
            pltpu.VMEM((2, dp_count, depth, half), jnp.bfloat16),
            pltpu.VMEM((2, dp_count - 1, depth, half), jnp.bfloat16),
            pltpu.VMEM((2, dp_count - 1, depth, half), jnp.bfloat16),
            pltpu.VMEM((seq_len, depth), jnp.float32),
            pltpu.VMEM((depth // HEAD_SIZE, seq_len, seq_len), jnp.float32),
            pltpu.VMEM((seq_len, depth), jnp.bfloat16),
            pltpu.VMEM((depth, seq_len), jnp.bfloat16),
            pltpu.VMEM((2, seq_len, HEAD_SIZE), jnp.float32),
            pltpu.VMEM((2, seq_len // 2, HEAD_SIZE), jnp.float32),
            dma((2, dp_count)),
            dma((2,)),
            dma((2, dp_count)),
            dma((2, dp_count)),
            dma((far, 2, dp_count)),
            dma((far, 2, dp_count)),
            dma((far, 2, dp_count)),
            dma((far, 2, dp_count)),
            dma((2, dp_count - 1)),
            dma((2, dp_count - 1)),
            dma((2, dp_count - 1)),
            dma((2, dp_count - 1)),
            dma,
            dma,
        ],
        compiler_params=pltpu.CompilerParams(
            collective_id=0, has_side_effects=True, vmem_limit_bytes=60 * 1024 * 1024
        ),
        name="exchange",
    )(grad_out[0], out_weight, query_act[0], rotated_keys[0], value_input[0], doc_lengths)
    return (query_grad[None], key_grad[None, None], value_grad[None, None], weight_grad)


def solution(mesh):
    placed = (
        P("dp", None, "tensor"),
        P("dp", None, None),
        P("dp", None, None),
        P("dp", "tensor", None),
        P("tensor", "dp"),
        P("dp", None),
    )
    return jax.shard_map(
        shards,
        mesh=mesh,
        in_specs=placed,
        out_specs=(
            P("dp", None, "tensor"),
            P("dp", "tensor", None, None),
            P("dp", "tensor", None, None),
            P("tensor", "dp"),
        ),
        check_vma=False,
    )
```

```python
import functools

import jax
import jax.numpy as jnp
from jax import lax
from jax.experimental import pallas as pl
from jax.experimental.pallas import tpu as pltpu
from jax.sharding import PartitionSpec as P

HEAD_SIZE = 128


MESH = pl.DeviceIdType.MESH


def ring_place(index, count):
    odd = index % 2
    return (1 - odd) * (index // 2) + odd * (count - 1 - index // 2)


def ring_index(place, count):
    back = place // (count // 2)
    return (1 - back) * (2 * place) + back * (2 * (count - 1 - place) + 1)


def exchange_kernel(
    dp_count,
    tensor_count,
    grad_ref,
    weight_ref,
    query_full,
    key_full,
    value_full,
    lengths_ref,
    query_grad_ref,
    key_grad_ref,
    value_grad_ref,
    weight_grad_ref,
    grads,
    weights,
    sums_out,
    sums_in,
    accum,
    query_ref,
    key_ref,
    value_ref,
    probs,
    dscores,
    outs,
    outs_t,
    kv_grads,
    kv_in,
    own_sem,
    own_weight_sem,
    near_send,
    near_recv,
    far_send,
    far_recv,
    pass_send,
    pass_recv,
    weight_send,
    weight_recv,
    sum_send,
    sum_recv,
    kv_send,
    kv_recv,
    load_sem,
):
    dp_index = lax.axis_index("dp")
    tensor_index = lax.axis_index("tensor")
    chip_count = tensor_count // 2
    chip, core = tensor_index // 2, tensor_index % 2
    partner = chip * 2 + 1 - core
    place = ring_place(dp_index, dp_count)
    ring = (
        ring_index((place + 1) % dp_count, dp_count),
        ring_index((place + dp_count - 1) % dp_count, dp_count),
    )
    rows = grad_ref.shape[0]
    half = weight_ref.shape[1] // 2
    last = dp_count - 1
    seq_len, depth = query_full.shape
    heads = depth // HEAD_SIZE
    half_rows = seq_len // 2
    score_scale = HEAD_SIZE ** (-0.5)
    lead = min(2, dp_count - 2)
    kv_columns = pl.ds(pl.multiple_of(tensor_index // 2 * HEAD_SIZE, HEAD_SIZE), HEAD_SIZE)
    far_chips = [(chip + away) % chip_count for away in range(1, chip_count)]

    def place_rows(index):
        return pl.ds(pl.multiple_of(index * rows, rows), rows)

    def columns(side, step):
        if side == 0:
            owner = ring_index((place + 2 * dp_count - 1 - step) % dp_count, dp_count)
        else:
            owner = ring_index((place + 1 + step) % dp_count, dp_count)
        return pl.ds(pl.multiple_of(owner * (2 * half) + side * half, half), half)

    def own_copy(side, step):
        return pltpu.make_async_copy(
            grad_ref.at[:, columns(side, step)],
            grads.at[side, step, place_rows(tensor_index)],
            own_sem.at[side, step],
        )

    def own_weight(side):
        return pltpu.make_async_copy(
            weight_ref.at[:, pl.ds(side * half, half)],
            weights.at[side, last],
            own_weight_sem.at[side],
        )

    def near_copy(side, step):
        return pltpu.make_async_remote_copy(
            grad_ref.at[:, columns(side, step)],
            grads.at[side, step, place_rows(tensor_index)],
            near_send.at[side, step],
            near_recv.at[side, step],
            device_id=(dp_index, partner),
            device_id_type=MESH,
        )

    def far_copy(away, side, step):
        return pltpu.make_async_remote_copy(
            grad_ref.at[:, columns(side, step)],
            grads.at[side, step, place_rows(tensor_index)],
            far_send.at[away, side, step],
            far_recv.at[away, side, step],
            device_id=(dp_index, far_chips[away] * 2 + core),
            device_id_type=MESH,
        )

    def pass_copy(away, side, step):
        source = (chip + chip_count - 1 - away) % chip_count * 2 + core
        block = grads.at[side, step, place_rows(source)]
        return pltpu.make_async_remote_copy(
            block,
            block,
            pass_send.at[away, side, step],
            pass_recv.at[away, side, step],
            device_id=(dp_index, partner),
            device_id_type=MESH,
        )

    def weight_copy(side, hop):
        if isinstance(hop, int) and hop == 0:
            source = weight_ref.at[:, pl.ds(side * half, half)]
        else:
            source = weights.at[side, hop - 1]
        return pltpu.make_async_remote_copy(
            source,
            weights.at[side, hop],
            weight_send.at[side, hop],
            weight_recv.at[side, hop],
            device_id=(ring[side], tensor_index),
            device_id_type=MESH,
        )

    def sum_copy(side, step):
        return pltpu.make_async_remote_copy(
            sums_out.at[side, step],
            sums_in.at[side, step],
            sum_send.at[side, step],
            sum_recv.at[side, step],
            device_id=(ring[side], tensor_index),
            device_id_type=MESH,
        )

    loads = [
        pltpu.make_async_copy(query_full, query_ref, load_sem.at[0]),
        pltpu.make_async_copy(key_full.at[:, kv_columns], key_ref, load_sem.at[1]),
        pltpu.make_async_copy(value_full.at[:, kv_columns], value_ref, load_sem.at[2]),
    ]
    for load in loads:
        load.start()

    targets = [(dp_index, partner), (ring[0], tensor_index), (ring[1], tensor_index)]
    targets += [(dp_index, other * 2 + core) for other in far_chips]
    barrier = pltpu.get_barrier_semaphore()
    for target in targets:
        pl.semaphore_signal(barrier, inc=1, device_id=target, device_id_type=MESH)
    pl.semaphore_wait(barrier, len(targets))

    def far_start(step):
        for side in (0, 1):
            for away in range(chip_count - 1):
                far_copy(away, side, step).start()

    far_start(0)
    for side in (0, 1):
        weight_copy(side, 0).start()
        own_weight(side).start()

    @pl.loop(1, dp_count)
    def _(step):
        far_start(step)

    @pl.loop(0, dp_count)
    def _(step):
        for side in (0, 1):
            near_copy(side, step).start()
            own_copy(side, step).start()

    kv_copy = pltpu.make_async_remote_copy(
        kv_grads.at[:, pl.ds(pl.multiple_of((1 - core) * half_rows, half_rows), half_rows)],
        kv_in,
        kv_send,
        kv_recv,
        device_id=(dp_index, partner),
        device_id_type=MESH,
    )
    accum[...] = jnp.zeros_like(accum)
    kv_grads[...] = jnp.zeros_like(kv_grads)
    nt = (((1,), (1,)), ((), ()))
    tn = (((0,), (0,)), ((), ()))

    def dot(left, right, dims):
        return lax.dot_general(left, right, dims, preferred_element_type=jnp.float32)

    def forward(block, size):
        here = pl.ds(pl.multiple_of(block * size, size), size)
        query_places = block * size + lax.broadcasted_iota(jnp.int32, (size, 1), 0)
        key_places = lax.broadcasted_iota(jnp.int32, (size, seq_len), 1)
        doc_start = jnp.zeros((size, 1), jnp.int32)
        doc_end = jnp.int32(0)
        for doc in range(lengths_ref.shape[1]):
            doc_end = doc_end + lengths_ref[0, doc]
            doc_start = jnp.where(query_places >= doc_end, doc_end, doc_start)
        allowed = (key_places >= doc_start) & (key_places <= query_places)
        keys, values = key_ref[...], value_ref[...]
        for head in range(heads):
            lanes = slice(head * HEAD_SIZE, (head + 1) * HEAD_SIZE)
            scores = dot(query_ref[here, lanes], keys, nt) * score_scale
            scores = jnp.where(allowed, scores, -jnp.inf)
            row_max = jnp.max(scores, axis=1, keepdims=True)
            total = jnp.sum(jnp.exp(scores - row_max), axis=1, keepdims=True)
            prob = jnp.exp(scores - (row_max + jnp.log(total)))
            probs[head, here] = prob
            out = jnp.dot(prob.astype(jnp.bfloat16), values, preferred_element_type=jnp.float32)
            outs[here, lanes] = out.astype(jnp.bfloat16)
            outs_t[lanes, here] = out.T.astype(jnp.bfloat16)

    def score_grads(block):
        here = place_rows(block)
        for head in range(heads):
            lanes = slice(head * HEAD_SIZE, (head + 1) * HEAD_SIZE)
            grad = accum[here, lanes].astype(jnp.bfloat16)
            delta = jnp.sum(
                grad.astype(jnp.float32) * outs[here, lanes].astype(jnp.float32), axis=1, keepdims=True
            )
            prob = probs[head, here]
            dscore = prob * (dot(grad, value_ref[...], nt) - delta) * score_scale
            dscores[head, here] = dscore.astype(jnp.bfloat16)

    def chip_rows(owner_chip):
        return pl.ds(pl.multiple_of(owner_chip * (2 * rows), 2 * rows), 2 * rows)

    def kv_part(owner_chip, part):
        here = chip_rows(owner_chip)
        to = pl.ds(pl.multiple_of(part * half_rows, half_rows), half_rows)
        key_total, value_total = kv_grads[0, to], kv_grads[1, to]
        for head in range(heads):
            lanes = slice(head * HEAD_SIZE, (head + 1) * HEAD_SIZE)
            key_total += dot(dscores[head, here, to], query_ref[here, lanes], tn)
            value_total += dot(
                probs[head, here, to].astype(jnp.bfloat16),
                accum[here, lanes].astype(jnp.bfloat16),
                tn,
            )
        kv_grads[0, to] = key_total
        kv_grads[1, to] = value_total

    def query_part(owner_chip):
        here = chip_rows(owner_chip)
        for head in range(heads):
            lanes = slice(head * HEAD_SIZE, (head + 1) * HEAD_SIZE)
            query_grad_ref[here, lanes] = jnp.dot(
                dscores[head, here], key_ref[...], preferred_element_type=jnp.float32
            ).astype(jnp.bfloat16)

    def project(owner_chip, step):
        here = chip_rows(owner_chip)
        total = accum[here]
        for side in (0, 1):
            total += dot(grads[side, step, here], weights[side, step], nt)
        accum[here] = total

    def local_step(step):
        for side in (0, 1):
            own_copy(side, step).wait()
            near_copy(side, step).wait_recv()
        project(chip, step)

    def weight_step(hop, send):
        for side in (0, 1):
            weight_copy(side, hop).wait_recv()
            if send:
                weight_copy(side, hop + 1).start()

    def far_step(step):
        for side in (0, 1):
            for away in range(chip_count - 1):
                far_copy(away, side, step).wait_recv()
                pass_copy(away, side, step).start()
        for side in (0, 1):
            for away in range(chip_count - 1):
                pass_copy(away, side, step).wait_recv()

    def sum_step(step, first, final):
        for side in (0, 1):
            part = jnp.dot(
                outs_t[...], grads[side, step], preferred_element_type=jnp.float32
            )
            if not first:
                sum_copy(side, step - 1).wait_recv()
                part = part + sums_in[side, step - 1].astype(jnp.float32)
            if final:
                weight_grad_ref[:, side * half : (side + 1) * half] = part
            else:
                sums_out[side, step] = part.astype(jnp.bfloat16)
                sum_copy(side, step).start()

    def far_project(step):
        for other in far_chips:
            project(other, step)

    for load in loads:
        load.wait()
    block_rows = min(256, seq_len)
    blocks = seq_len // block_rows

    @pl.loop(0, blocks // 2)
    def _(block):
        forward(block, block_rows)

    weight_step(0, dp_count > 2)

    @pl.loop(blocks // 2, blocks)
    def _(block):
        forward(block, block_rows)

    for hop in range(1, lead):
        weight_step(hop, hop < last - 1)
    for side in (0, 1):
        own_weight(side).wait()
    local_step(last)
    for step in range(lead):
        local_step(step)

    def step_with_weights(step, first, send):
        weight_step(step + lead, send)
        local_step(step + lead)
        far_step(step)
        sum_step(step, first, False)
        far_project(step)

    step_with_weights(0, True, lead < last - 1)

    @pl.loop(1, last - 1 - lead)
    def _(step):
        step_with_weights(step, False, True)

    if last - 1 - lead > 0:
        step_with_weights(last - 1 - lead, False, False)

    for step in range(last - lead, last):
        far_step(step)
        sum_step(step, False, False)
        far_project(step)
        if step == last - lead:

            @pl.loop(0, 2)
            def _(block):
                score_grads(chip * 2 + block)

            kv_part(chip, 0)
            kv_part(chip, 1)
            query_part(chip)

    far_step(last)
    far_project(last)

    @pl.loop(0, tensor_count - 2)
    def _(block):
        score_grads((chip * 2 + 2 + block) % tensor_count)

    for other in far_chips:
        kv_part(other, 1 - core)
    kv_copy.start()
    for other in far_chips:
        kv_part(other, core)
        query_part(other)
    sum_step(last, False, True)
    kv_copy.wait()
    mine = pl.ds(pl.multiple_of(core * half_rows, half_rows), half_rows)
    key_grad_ref[...] = (kv_grads[0, mine] + kv_in[0]).astype(jnp.bfloat16)
    value_grad_ref[...] = (kv_grads[1, mine] + kv_in[1]).astype(jnp.bfloat16)

    @pl.loop(0, dp_count)
    def _(step):
        for side in (0, 1):
            near_copy(side, step).wait_send()
            for away in range(chip_count - 1):
                far_copy(away, side, step).wait_send()
                pass_copy(away, side, step).wait_send()

    @pl.loop(1, dp_count - 1)
    def _(step):
        for side in (0, 1):
            weight_copy(side, step).wait_send()
            sum_copy(side, step).wait_send()

    for side in (0, 1):
        weight_copy(side, 0).wait_send()
        sum_copy(side, 0).wait_send()


def finish_kernel(*refs):
    count = (len(refs) - 2) // 3
    sources, results, held = refs[:count], refs[count : 2 * count], refs[2 * count : 3 * count]
    in_sem, out_sem = refs[3 * count :]
    takes = [pltpu.make_async_copy(sources[i], held[i], in_sem.at[i]) for i in range(count)]
    puts = [pltpu.make_async_copy(held[i], results[i], out_sem.at[i]) for i in range(count)]
    for take in takes:
        take.start()
    for take, put in zip(takes, puts):
        take.wait()
        put.start()
    for put in puts:
        put.wait()


def finish(*values):
    anywhere = pl.BlockSpec(memory_space=pl.ANY)
    dma = pltpu.SemaphoreType.DMA
    return pl.pallas_call(
        finish_kernel,
        out_shape=tuple(jax.ShapeDtypeStruct(value.shape, value.dtype) for value in values),
        in_specs=[anywhere] * len(values),
        out_specs=(anywhere,) * len(values),
        scratch_shapes=[pltpu.VMEM(value.shape, value.dtype) for value in values]
        + [dma((len(values),)), dma((len(values),))],
        compiler_params=pltpu.CompilerParams(vmem_limit_bytes=62 * 1024 * 1024),
        name="finish",
    )(*values)


def shards(query_act, rotated_keys, value_input, grad_out, out_weight, doc_lengths):
    dp_count, tensor_count = lax.axis_size("dp"), lax.axis_size("tensor")
    far = tensor_count // 2 - 1
    seq_len = query_act.shape[1]
    depth, width = out_weight.shape
    half = width // 2
    dma = pltpu.SemaphoreType.DMA
    vmem = pl.BlockSpec(memory_space=pltpu.VMEM)
    anywhere = pl.BlockSpec(memory_space=pl.ANY)
    kv_shape = jax.ShapeDtypeStruct((seq_len // 2, HEAD_SIZE), jnp.bfloat16)
    query_grad, key_grad, value_grad, weight_grad = pl.pallas_call(
        functools.partial(exchange_kernel, dp_count, tensor_count),
        out_shape=(
            jax.ShapeDtypeStruct((seq_len, depth), jnp.bfloat16),
            kv_shape,
            kv_shape,
            jax.ShapeDtypeStruct((depth, width), jnp.float32),
        ),
        in_specs=[
            anywhere,
            anywhere,
            anywhere,
            anywhere,
            anywhere,
            pl.BlockSpec(memory_space=pltpu.SMEM),
        ],
        out_specs=(vmem, vmem, vmem, vmem),
        scratch_shapes=[
            pltpu.VMEM((2, dp_count, seq_len, half), jnp.bfloat16),
            pltpu.VMEM((2, dp_count, depth, half), jnp.bfloat16),
            pltpu.VMEM((2, dp_count - 1, depth, half), jnp.bfloat16),
            pltpu.VMEM((2, dp_count - 1, depth, half), jnp.bfloat16),
            pltpu.VMEM((seq_len, depth), jnp.float32),
            pltpu.VMEM((seq_len, depth), jnp.bfloat16),
            pltpu.VMEM((seq_len, HEAD_SIZE), jnp.bfloat16),
            pltpu.VMEM((seq_len, HEAD_SIZE), jnp.bfloat16),
            pltpu.VMEM((depth // HEAD_SIZE, seq_len, seq_len), jnp.float32),
            pltpu.VMEM((depth // HEAD_SIZE, seq_len, seq_len), jnp.bfloat16),
            pltpu.VMEM((seq_len, depth), jnp.bfloat16),
            pltpu.VMEM((depth, seq_len), jnp.bfloat16),
            pltpu.VMEM((2, seq_len, HEAD_SIZE), jnp.float32),
            pltpu.VMEM((2, seq_len // 2, HEAD_SIZE), jnp.float32),
            dma((2, dp_count)),
            dma((2,)),
            dma((2, dp_count)),
            dma((2, dp_count)),
            dma((far, 2, dp_count)),
            dma((far, 2, dp_count)),
            dma((far, 2, dp_count)),
            dma((far, 2, dp_count)),
            dma((2, dp_count - 1)),
            dma((2, dp_count - 1)),
            dma((2, dp_count - 1)),
            dma((2, dp_count - 1)),
            dma,
            dma,
            dma((3,)),
        ],
        compiler_params=pltpu.CompilerParams(
            collective_id=0, has_side_effects=True, vmem_limit_bytes=60 * 1024 * 1024
        ),
        name="exchange",
    )(grad_out[0], out_weight, query_act[0], rotated_keys[0], value_input[0], doc_lengths)
    query_grad, key_grad, value_grad, weight_grad = finish(
        query_grad, key_grad, value_grad, weight_grad
    )
    return (query_grad[None], key_grad[None, None], value_grad[None, None], weight_grad)


def solution(mesh):
    placed = (
        P("dp", None, "tensor"),
        P("dp", None, None),
        P("dp", None, None),
        P("dp", "tensor", None),
        P("tensor", "dp"),
        P("dp", None),
    )
    return jax.shard_map(
        shards,
        mesh=mesh,
        in_specs=placed,
        out_specs=(
            P("dp", None, "tensor"),
            P("dp", "tensor", None, None),
            P("dp", "tensor", None, None),
            P("tensor", "dp"),
        ),
        check_vma=False,
    )
```

```python
import functools

import jax
import jax.numpy as jnp
from jax import lax
from jax.experimental import pallas as pl
from jax.experimental.pallas import tpu as pltpu
from jax.sharding import PartitionSpec as P

HEAD_SIZE = 128


MESH = pl.DeviceIdType.MESH


def ring_place(index, count):
    odd = index % 2
    return (1 - odd) * (index // 2) + odd * (count - 1 - index // 2)


def ring_index(place, count):
    back = place // (count // 2)
    return (1 - back) * (2 * place) + back * (2 * (count - 1 - place) + 1)


def exchange_kernel(
    dp_count,
    tensor_count,
    grad_ref,
    weight_ref,
    query_full,
    key_full,
    value_full,
    lengths_ref,
    query_grad_out,
    key_grad_ref,
    value_grad_ref,
    weight_grad_out,
    grads,
    weights,
    sums_out,
    sums_in,
    accum,
    query_ref,
    key_ref,
    value_ref,
    query_grad_ref,
    weight_grad_ref,
    probs,
    probs_t,
    dscores,
    outs,
    outs_t,
    kv_grads,
    kv_in,
    own_sem,
    own_weight_sem,
    near_send,
    near_recv,
    far_send,
    far_recv,
    pass_send,
    pass_recv,
    weight_send,
    weight_recv,
    sum_send,
    sum_recv,
    kv_send,
    kv_recv,
    load_sem,
    out_sem,
):
    dp_index = lax.axis_index("dp")
    tensor_index = lax.axis_index("tensor")
    chip_count = tensor_count // 2
    chip, core = tensor_index // 2, tensor_index % 2
    partner = chip * 2 + 1 - core
    place = ring_place(dp_index, dp_count)
    ring = (
        ring_index((place + 1) % dp_count, dp_count),
        ring_index((place + dp_count - 1) % dp_count, dp_count),
    )
    rows = grad_ref.shape[0]
    half = weight_ref.shape[1] // 2
    last = dp_count - 1
    seq_len, depth = query_full.shape
    heads = depth // HEAD_SIZE
    half_rows = seq_len // 2
    score_scale = HEAD_SIZE ** (-0.5)
    lead = min(2, dp_count - 2)
    kv_columns = pl.ds(pl.multiple_of(tensor_index // 2 * HEAD_SIZE, HEAD_SIZE), HEAD_SIZE)
    far_chips = [(chip + away) % chip_count for away in range(1, chip_count)]

    def place_rows(index):
        return pl.ds(pl.multiple_of(index * rows, rows), rows)

    def columns(side, step):
        if side == 0:
            owner = ring_index((place + 2 * dp_count - 1 - step) % dp_count, dp_count)
        else:
            owner = ring_index((place + 1 + step) % dp_count, dp_count)
        return pl.ds(pl.multiple_of(owner * (2 * half) + side * half, half), half)

    def own_copy(side, step):
        return pltpu.make_async_copy(
            grad_ref.at[:, columns(side, step)],
            grads.at[side, step, place_rows(tensor_index)],
            own_sem.at[side, step],
        )

    def own_weight(side):
        return pltpu.make_async_copy(
            weight_ref.at[:, pl.ds(side * half, half)],
            weights.at[side, last],
            own_weight_sem.at[side],
        )

    def near_copy(side, step):
        return pltpu.make_async_remote_copy(
            grad_ref.at[:, columns(side, step)],
            grads.at[side, step, place_rows(tensor_index)],
            near_send.at[side, step],
            near_recv.at[side, step],
            device_id=(dp_index, partner),
            device_id_type=MESH,
        )

    def far_copy(away, side, step):
        return pltpu.make_async_remote_copy(
            grad_ref.at[:, columns(side, step)],
            grads.at[side, step, place_rows(tensor_index)],
            far_send.at[away, side, step],
            far_recv.at[away, side, step],
            device_id=(dp_index, far_chips[away] * 2 + core),
            device_id_type=MESH,
        )

    def pass_copy(away, side, step):
        source = (chip + chip_count - 1 - away) % chip_count * 2 + core
        block = grads.at[side, step, place_rows(source)]
        return pltpu.make_async_remote_copy(
            block,
            block,
            pass_send.at[away, side, step],
            pass_recv.at[away, side, step],
            device_id=(dp_index, partner),
            device_id_type=MESH,
        )

    def weight_copy(side, hop):
        if isinstance(hop, int) and hop == 0:
            source = weight_ref.at[:, pl.ds(side * half, half)]
        else:
            source = weights.at[side, hop - 1]
        return pltpu.make_async_remote_copy(
            source,
            weights.at[side, hop],
            weight_send.at[side, hop],
            weight_recv.at[side, hop],
            device_id=(ring[side], tensor_index),
            device_id_type=MESH,
        )

    def sum_copy(side, step):
        return pltpu.make_async_remote_copy(
            sums_out.at[side, step],
            sums_in.at[side, step],
            sum_send.at[side, step],
            sum_recv.at[side, step],
            device_id=(ring[side], tensor_index),
            device_id_type=MESH,
        )

    loads = [
        pltpu.make_async_copy(query_full, query_ref, load_sem.at[0]),
        pltpu.make_async_copy(key_full.at[:, kv_columns], key_ref, load_sem.at[1]),
        pltpu.make_async_copy(value_full.at[:, kv_columns], value_ref, load_sem.at[2]),
    ]
    for load in loads:
        load.start()

    targets = [(dp_index, partner), (ring[0], tensor_index), (ring[1], tensor_index)]
    targets += [(dp_index, other * 2 + core) for other in far_chips]
    barrier = pltpu.get_barrier_semaphore()
    for target in targets:
        pl.semaphore_signal(barrier, inc=1, device_id=target, device_id_type=MESH)
    pl.semaphore_wait(barrier, len(targets))

    def far_start(step):
        for side in (0, 1):
            for away in range(chip_count - 1):
                far_copy(away, side, step).start()

    far_start(0)
    for side in (0, 1):
        weight_copy(side, 0).start()
        own_weight(side).start()

    @pl.loop(1, dp_count)
    def _(step):
        far_start(step)

    @pl.loop(0, dp_count)
    def _(step):
        for side in (0, 1):
            near_copy(side, step).start()
            own_copy(side, step).start()

    kv_copy = pltpu.make_async_remote_copy(
        kv_grads.at[:, pl.ds(pl.multiple_of((1 - core) * half_rows, half_rows), half_rows)],
        kv_in,
        kv_send,
        kv_recv,
        device_id=(dp_index, partner),
        device_id_type=MESH,
    )
    accum[...] = jnp.zeros_like(accum)
    kv_grads[...] = jnp.zeros_like(kv_grads)
    nt = (((1,), (1,)), ((), ()))
    tn = (((0,), (0,)), ((), ()))
    nn = (((1,), (0,)), ((), ()))
    weight_put = pltpu.make_async_copy(weight_grad_ref, weight_grad_out, out_sem.at[chip_count])

    def dot(left, right, dims):
        return lax.dot_general(left, right, dims, preferred_element_type=jnp.float32)

    def forward(block, size):
        here = pl.ds(pl.multiple_of(block * size, size), size)
        query_places = block * size + lax.broadcasted_iota(jnp.int32, (size, 1), 0)
        key_places = lax.broadcasted_iota(jnp.int32, (size, seq_len), 1)
        doc_start = jnp.zeros((size, 1), jnp.int32)
        doc_end = jnp.int32(0)
        for doc in range(lengths_ref.shape[1]):
            doc_end = doc_end + lengths_ref[0, doc]
            doc_start = jnp.where(query_places >= doc_end, doc_end, doc_start)
        allowed = (key_places >= doc_start) & (key_places <= query_places)
        keys, values = key_ref[...], value_ref[...]
        for head in range(heads):
            lanes = slice(head * HEAD_SIZE, (head + 1) * HEAD_SIZE)
            scores = dot(query_ref[here, lanes], keys, nt) * score_scale
            scores = jnp.where(allowed, scores, -jnp.inf)
            row_max = jnp.max(scores, axis=1, keepdims=True)
            total = jnp.sum(jnp.exp(scores - row_max), axis=1, keepdims=True)
            prob = jnp.exp(scores - (row_max + jnp.log(total)))
            probs[head, here] = prob
            out = jnp.dot(prob.astype(jnp.bfloat16), values, preferred_element_type=jnp.float32)
            outs[here, lanes] = out.astype(jnp.bfloat16)
            outs_t[lanes, here] = out.T.astype(jnp.bfloat16)

    def score_grads(block):
        here = place_rows(block)
        for head in range(heads):
            lanes = slice(head * HEAD_SIZE, (head + 1) * HEAD_SIZE)
            grad = accum[here, lanes].astype(jnp.bfloat16)
            delta = jnp.sum(
                grad.astype(jnp.float32) * outs[here, lanes].astype(jnp.float32), axis=1, keepdims=True
            )
            prob = probs[head, here]
            dscore = prob * (dot(grad, value_ref[...], nt) - delta) * score_scale
            dscores[head, here] = dscore.astype(jnp.bfloat16)

    def chip_rows(owner_chip):
        return pl.ds(pl.multiple_of(owner_chip * (2 * rows), 2 * rows), 2 * rows)

    def kv_part(owner_chip, part):
        here = chip_rows(owner_chip)
        to = pl.ds(pl.multiple_of(part * half_rows, half_rows), half_rows)
        key_total, value_total = kv_grads[0, to], kv_grads[1, to]
        for head in range(heads):
            lanes = slice(head * HEAD_SIZE, (head + 1) * HEAD_SIZE)
            key_total += dot(dscores[head, here, to], query_ref[here, lanes], tn)
            value_total += dot(
                probs_t[owner_chip, head, to],
                accum[here, lanes].astype(jnp.bfloat16),
                nn,
            )
        kv_grads[0, to] = key_total
        kv_grads[1, to] = value_total

    def transpose_probs(owner_chip):
        for head in range(heads):
            probs_t[owner_chip, head] = probs[head, chip_rows(owner_chip)].T.astype(jnp.bfloat16)

    def query_put(owner_chip):
        here = chip_rows(owner_chip)
        return pltpu.make_async_copy(
            query_grad_ref.at[here], query_grad_out.at[here], out_sem.at[owner_chip]
        )

    def query_part(owner_chip):
        here = chip_rows(owner_chip)
        for head in range(heads):
            lanes = slice(head * HEAD_SIZE, (head + 1) * HEAD_SIZE)
            query_grad_ref[here, lanes] = jnp.dot(
                dscores[head, here], key_ref[...], preferred_element_type=jnp.float32
            ).astype(jnp.bfloat16)
        query_put(owner_chip).start()

    def project(owner_chip, step):
        here = chip_rows(owner_chip)
        total = accum[here]
        for side in (0, 1):
            total += dot(grads[side, step, here], weights[side, step], nt)
        accum[here] = total

    def local_step(step):
        for side in (0, 1):
            own_copy(side, step).wait()
            near_copy(side, step).wait_recv()
        project(chip, step)

    def weight_step(hop, send):
        for side in (0, 1):
            weight_copy(side, hop).wait_recv()
            if send:
                weight_copy(side, hop + 1).start()

    def far_step(step):
        for side in (0, 1):
            for away in range(chip_count - 1):
                far_copy(away, side, step).wait_recv()
                pass_copy(away, side, step).start()
        for side in (0, 1):
            for away in range(chip_count - 1):
                pass_copy(away, side, step).wait_recv()

    def sum_step(step, first, final):
        for side in (0, 1):
            part = jnp.dot(
                outs_t[...], grads[side, step], preferred_element_type=jnp.float32
            )
            if not first:
                sum_copy(side, step - 1).wait_recv()
                part = part + sums_in[side, step - 1].astype(jnp.float32)
            if final:
                weight_grad_ref[:, side * half : (side + 1) * half] = part
            else:
                sums_out[side, step] = part.astype(jnp.bfloat16)
                sum_copy(side, step).start()

    def far_project(step):
        for other in far_chips:
            project(other, step)

    for load in loads:
        load.wait()
    block_rows = min(256, seq_len)
    blocks = seq_len // block_rows

    @pl.loop(0, blocks // 2)
    def _(block):
        forward(block, block_rows)

    weight_step(0, dp_count > 2)

    @pl.loop(blocks // 2, blocks)
    def _(block):
        forward(block, block_rows)

    for hop in range(1, lead):
        weight_step(hop, hop < last - 1)
    for side in (0, 1):
        own_weight(side).wait()
    local_step(last)
    for step in range(lead):
        local_step(step)

    def step_with_weights(step, first, send):
        weight_step(step + lead, send)
        local_step(step + lead)
        far_step(step)
        sum_step(step, first, False)
        far_project(step)

    step_with_weights(0, True, lead < last - 1)

    @pl.loop(1, last - 1 - lead)
    def _(step):
        step_with_weights(step, False, True)

    if last - 1 - lead > 0:
        step_with_weights(last - 1 - lead, False, False)

    @pl.loop(0, chip_count)
    def _(owner_chip):
        transpose_probs(owner_chip)

    for step in range(last - lead, last):
        far_step(step)
        sum_step(step, False, False)
        far_project(step)
        if step == last - lead:

            @pl.loop(0, 2)
            def _(block):
                score_grads(chip * 2 + block)

            kv_part(chip, 0)
            kv_part(chip, 1)
            query_part(chip)

    far_step(last)
    far_project(last)

    @pl.loop(0, tensor_count - 2)
    def _(block):
        score_grads((chip * 2 + 2 + block) % tensor_count)

    for other in far_chips:
        kv_part(other, 1 - core)
    kv_copy.start()
    sum_step(last, False, True)
    weight_put.start()
    for other in far_chips:
        query_part(other)
    for other in far_chips:
        kv_part(other, core)
    kv_copy.wait()
    mine = pl.ds(pl.multiple_of(core * half_rows, half_rows), half_rows)
    key_grad_ref[...] = (kv_grads[0, mine] + kv_in[0]).astype(jnp.bfloat16)
    value_grad_ref[...] = (kv_grads[1, mine] + kv_in[1]).astype(jnp.bfloat16)

    @pl.loop(0, dp_count)
    def _(step):
        for side in (0, 1):
            near_copy(side, step).wait_send()
            for away in range(chip_count - 1):
                far_copy(away, side, step).wait_send()
                pass_copy(away, side, step).wait_send()

    @pl.loop(1, dp_count - 1)
    def _(step):
        for side in (0, 1):
            weight_copy(side, step).wait_send()
            sum_copy(side, step).wait_send()

    weight_put.wait()

    @pl.loop(0, chip_count)
    def _(owner_chip):
        query_put(owner_chip).wait()

    for side in (0, 1):
        weight_copy(side, 0).wait_send()
        sum_copy(side, 0).wait_send()


def finish_kernel(*refs):
    count = (len(refs) - 2) // 3
    sources, results, held = refs[:count], refs[count : 2 * count], refs[2 * count : 3 * count]
    in_sem, out_sem = refs[3 * count :]
    takes = [pltpu.make_async_copy(sources[i], held[i], in_sem.at[i]) for i in range(count)]
    puts = [pltpu.make_async_copy(held[i], results[i], out_sem.at[i]) for i in range(count)]
    for take in takes:
        take.start()
    for take, put in zip(takes, puts):
        take.wait()
        put.start()
    for put in puts:
        put.wait()


def finish(*values):
    anywhere = pl.BlockSpec(memory_space=pl.ANY)
    dma = pltpu.SemaphoreType.DMA
    return pl.pallas_call(
        finish_kernel,
        out_shape=tuple(jax.ShapeDtypeStruct(value.shape, value.dtype) for value in values),
        in_specs=[anywhere] * len(values),
        out_specs=(anywhere,) * len(values),
        scratch_shapes=[pltpu.VMEM(value.shape, value.dtype) for value in values]
        + [dma((len(values),)), dma((len(values),))],
        compiler_params=pltpu.CompilerParams(vmem_limit_bytes=62 * 1024 * 1024),
        name="finish",
    )(*values)


def shards(query_act, rotated_keys, value_input, grad_out, out_weight, doc_lengths):
    dp_count, tensor_count = lax.axis_size("dp"), lax.axis_size("tensor")
    far = tensor_count // 2 - 1
    seq_len = query_act.shape[1]
    depth, width = out_weight.shape
    half = width // 2
    dma = pltpu.SemaphoreType.DMA
    vmem = pl.BlockSpec(memory_space=pltpu.VMEM)
    anywhere = pl.BlockSpec(memory_space=pl.ANY)
    kv_shape = jax.ShapeDtypeStruct((seq_len // 2, HEAD_SIZE), jnp.bfloat16)
    query_grad, key_grad, value_grad, weight_grad = pl.pallas_call(
        functools.partial(exchange_kernel, dp_count, tensor_count),
        out_shape=(
            jax.ShapeDtypeStruct((seq_len, depth), jnp.bfloat16),
            kv_shape,
            kv_shape,
            jax.ShapeDtypeStruct((depth, width), jnp.float32),
        ),
        in_specs=[
            anywhere,
            anywhere,
            anywhere,
            anywhere,
            anywhere,
            pl.BlockSpec(memory_space=pltpu.SMEM),
        ],
        out_specs=(anywhere, vmem, vmem, anywhere),
        scratch_shapes=[
            pltpu.VMEM((2, dp_count, seq_len, half), jnp.bfloat16),
            pltpu.VMEM((2, dp_count, depth, half), jnp.bfloat16),
            pltpu.VMEM((2, dp_count - 1, depth, half), jnp.bfloat16),
            pltpu.VMEM((2, dp_count - 1, depth, half), jnp.bfloat16),
            pltpu.VMEM((seq_len, depth), jnp.float32),
            pltpu.VMEM((seq_len, depth), jnp.bfloat16),
            pltpu.VMEM((seq_len, HEAD_SIZE), jnp.bfloat16),
            pltpu.VMEM((seq_len, HEAD_SIZE), jnp.bfloat16),
            pltpu.VMEM((seq_len, depth), jnp.bfloat16),
            pltpu.VMEM((depth, width), jnp.float32),
            pltpu.VMEM((depth // HEAD_SIZE, seq_len, seq_len), jnp.float32),
            pltpu.VMEM(
                (
                    tensor_count // 2,
                    depth // HEAD_SIZE,
                    seq_len,
                    seq_len // (tensor_count // 2),
                ),
                jnp.bfloat16,
            ),
            pltpu.VMEM((depth // HEAD_SIZE, seq_len, seq_len), jnp.bfloat16),
            pltpu.VMEM((seq_len, depth), jnp.bfloat16),
            pltpu.VMEM((depth, seq_len), jnp.bfloat16),
            pltpu.VMEM((2, seq_len, HEAD_SIZE), jnp.float32),
            pltpu.VMEM((2, seq_len // 2, HEAD_SIZE), jnp.float32),
            dma((2, dp_count)),
            dma((2,)),
            dma((2, dp_count)),
            dma((2, dp_count)),
            dma((far, 2, dp_count)),
            dma((far, 2, dp_count)),
            dma((far, 2, dp_count)),
            dma((far, 2, dp_count)),
            dma((2, dp_count - 1)),
            dma((2, dp_count - 1)),
            dma((2, dp_count - 1)),
            dma((2, dp_count - 1)),
            dma,
            dma,
            dma((3,)),
            dma((tensor_count // 2 + 1,)),
        ],
        compiler_params=pltpu.CompilerParams(
            collective_id=0, has_side_effects=True, vmem_limit_bytes=60 * 1024 * 1024
        ),
        name="exchange",
    )(grad_out[0], out_weight, query_act[0], rotated_keys[0], value_input[0], doc_lengths)
    query_grad, key_grad, value_grad, weight_grad = finish(
        query_grad, key_grad, value_grad, weight_grad
    )
    return (query_grad[None], key_grad[None, None], value_grad[None, None], weight_grad)


def solution(mesh):
    placed = (
        P("dp", None, "tensor"),
        P("dp", None, None),
        P("dp", None, None),
        P("dp", "tensor", None),
        P("tensor", "dp"),
        P("dp", None),
    )
    return jax.shard_map(
        shards,
        mesh=mesh,
        in_specs=placed,
        out_specs=(
            P("dp", None, "tensor"),
            P("dp", "tensor", None, None),
            P("dp", "tensor", None, None),
            P("tensor", "dp"),
        ),
        check_vma=False,
    )
```
